1024 devices in a mesh: seq: 128 (over x, y, core), head: 8 (over z).
Axes of the slice: x: 8, y: 8, z: 8, core: 2. Of those that a mesh axis runs over, the one named last changes fastest.
Arguments:
- queries: bfloat16 [16384, 8192], P('seq', 'head'), parts along dimension 1, may hold values from -12 to 12
- key_rows: bfloat16 [16384, 1024], P('seq', 'head'), parts along dimension 1, may hold values from -12 to 12
- value_rows: bfloat16 [16384, 1024], P('seq', 'head'), parts along dimension 1, may hold values from -6 to 6
- out_grad: bfloat16 [16384, 8192], P('seq', 'head'), parts along dimension 1, may hold values from -6 to 6
- doc_blocks: int32 [64], replicated, may hold values from 1 to 8, 128 in all
Outputs:
- attended: bfloat16 [16384, 8192], P('seq', 'head'), parts along dimension 1
- query_grad: bfloat16 [16384, 8192], P('seq', 'head'), parts along dimension 1
- key_grad: bfloat16 [16384, 1024], P('seq', 'head'), parts along dimension 1
- value_grad: bfloat16 [16384, 1024], P('seq', 'head'), parts along dimension 1
The draws below stay inside these ranges and needn't reach their ends.
There are 8 independent parts, one for each index of `head`. The reference program is written for one: setup_inputs(seed, part) draws one part's arguments, and reference() takes and returns one part's arrays. A program takes and returns all parts, laid end to end along the dimension named above; an argument that names none is the same for every part. Nothing has to cross between parts.
All inputs are finite; a program needn't handle non-finite values.
Results may differ from the reference program's by a relative error of at most 0.013.
Values may be sent and summed in bfloat16 or wider, within the bound.
A program may use at most 32 MiB of HBM per device.

```python
import math
import jax
import jax.numpy as jnp
import numpy as np
from jax import lax

HQ = 8
DH = 128
S_DEV = 128
BLOCK = 128
WIN = 8
TOKENS = 16384
DOCS = 64
N_SEQ = 128


def draw_queries(key, part):
    drawn = jnp.clip(jax.random.normal(jax.random.fold_in(key, 1), (TOKENS, HQ * DH), jnp.float32), -6.0, 6.0)
    return drawn.astype(jnp.bfloat16)


def draw_key_rows(key, part):
    drawn = jnp.clip(jax.random.normal(jax.random.fold_in(key, 2), (TOKENS, DH), jnp.float32), -6.0, 6.0)
    return drawn.astype(jnp.bfloat16)


def level_of(stream_key, shape, shards, least, high):
    level = 1.0
    for axis_at, parts in shards:
        steps = jax.random.uniform(jax.random.fold_in(jax.random.fold_in(stream_key, 6), axis_at), (parts,), jnp.float32, least / len(shards), high / len(shards))
        level = level * jnp.repeat(jnp.exp(steps), shape[axis_at] // parts).reshape((-1,) + (1,) * (len(shape) - 1 - axis_at))
    return level


def length_profile(number_of, total, limit, lean):
    portions = [(1 << 20) // math.isqrt(standing ** lean) + 1 for standing in range(2, number_of + 1)]
    surplus, holding = total - limit - (number_of - 1), [1] * (number_of - 1)
    while surplus > 0:
        free = [i for i in range(number_of - 1) if holding[i] < limit]
        mass, budget = sum([portions[i] for i in free]), surplus
        for i in free:
            addition = min(limit - holding[i], max(1, budget * portions[i] // mass), surplus)
            holding[i] = holding[i] + addition
            surplus = surplus - addition
    return np.array([limit] + holding)


def uneven_parts(own_key, count, total, bound, slope):
    if count == 2:
        one = jax.random.randint(own_key, (), max(1, total - bound), min(bound, total - 1) + 1)
        return jnp.stack([one, total - one])
    sizes = jnp.asarray(length_profile(count, total, bound, slope), jnp.int32)
    pairs = (count - 1) // 2
    donor, sink = sizes[1:1 + 2 * pairs:2], sizes[2:2 + 2 * pairs:2]
    slack = jnp.minimum(donor - 1, bound - sink)
    moved = jax.random.randint(jax.random.fold_in(own_key, 1), (pairs,), 0, 1 << 20) % (slack + 1)
    sizes = sizes.at[1:1 + 2 * pairs:2].set(donor - moved).at[2:2 + 2 * pairs:2].set(sink + moved)
    return sizes[jax.random.permutation(jax.random.fold_in(own_key, 2), count)]


def normal_values(key, shape, deviation, bound, shards=(), held_as=jnp.bfloat16):
    values = jax.random.normal(key, shape, jnp.float32) * deviation
    if len(shards) > 0:
        values = level_of(key, shape, shards, -0.22, 0.18) * values
    return jnp.clip(values, min=-bound, max=bound).astype(held_as)


def setup_inputs(seed: int = 0, part: int = 0) -> dict:
    splits = jax.random.split(jax.random.key(seed), 6)
    part_splits = jax.random.split(jax.random.fold_in(splits[5], part), 6)
    return {
        "queries": draw_queries(jax.random.fold_in(jax.random.fold_in(splits[5], part), 71), part),
        "key_rows": draw_key_rows(jax.random.fold_in(jax.random.fold_in(splits[5], part), 71), part),
        "value_rows": normal_values(part_splits[2], (TOKENS, DH), 1.0, 6.0, ((0, 128),)),
        "out_grad": normal_values(part_splits[3], (TOKENS, HQ * DH), 1.0, 6.0, ((0, 128),)),
        "doc_blocks": uneven_parts(splits[4], DOCS, TOKENS // BLOCK, (WIN - 1) * S_DEV // BLOCK + 1, 1).astype(jnp.int32),
    }


def doc_index(positions, ends):
    return jnp.sum((ends[None, :] <= positions[:, None]).astype(jnp.int32), axis=1)


def reference(queries, key_rows, value_rows, out_grad, doc_blocks):
    score_scale = DH ** -0.5
    ends = (BLOCK * jnp.cumsum(doc_blocks)).astype(jnp.int32)
    margin = (WIN - 1) * S_DEV
    keys_padded = jnp.concatenate([jnp.zeros((margin, DH), key_rows.dtype), key_rows], axis=0)
    values_padded = jnp.concatenate([jnp.zeros((margin, DH), value_rows.dtype), value_rows], axis=0)
    zero_index = jnp.zeros((), jnp.int32)

    def block_step(grads_padded, block_index):
        first = (block_index * S_DEV).astype(jnp.int32)
        query_block = lax.dynamic_slice_in_dim(queries, first, S_DEV, 0).reshape(S_DEV * HQ, DH)
        grad_block = lax.dynamic_slice_in_dim(out_grad, first, S_DEV, 0).reshape(S_DEV * HQ, DH)
        key_block = lax.dynamic_slice_in_dim(keys_padded, first, WIN * S_DEV, 0)
        value_block = lax.dynamic_slice_in_dim(values_padded, first, WIN * S_DEV, 0)
        query_pos = first + jnp.arange(S_DEV, dtype=jnp.int32)
        row_pos = jnp.repeat(query_pos, HQ)
        key_pos = first - margin + jnp.arange(WIN * S_DEV, dtype=jnp.int32)
        allowed = (key_pos[None, :] >= 0) & (key_pos[None, :] <= row_pos[:, None])
        allowed = allowed & (doc_index(key_pos, ends)[None, :] == doc_index(row_pos, ends)[:, None])
        scores = jnp.dot(query_block, key_block.T, preferred_element_type=jnp.float32) * score_scale
        row_max = jnp.max(jnp.where(allowed, scores, -jnp.inf), axis=1)
        row_total = jnp.sum(jnp.where(allowed, jnp.exp(scores - row_max[:, None]), 0.0), axis=1)
        lse = row_max + jnp.log(row_total)
        weights = jnp.where(allowed, jnp.exp(scores - lse[:, None]), 0.0)
        weights_bf = weights.astype(jnp.bfloat16)
        attended = jnp.dot(weights_bf, value_block, preferred_element_type=jnp.float32).astype(jnp.bfloat16)
        delta = jnp.sum(grad_block.astype(jnp.float32) * attended.astype(jnp.float32), axis=1)
        grad_weights = jnp.dot(grad_block, value_block.T, preferred_element_type=jnp.float32)
        grad_scores = (weights * (grad_weights - delta[:, None]) * score_scale).astype(jnp.bfloat16)
        query_grad = jnp.dot(grad_scores, key_block, preferred_element_type=jnp.float32).astype(jnp.bfloat16)
        key_part = jnp.dot(grad_scores.T, query_block, preferred_element_type=jnp.float32)
        value_part = jnp.dot(weights_bf.T, grad_block, preferred_element_type=jnp.float32)
        old_part = lax.dynamic_slice(grads_padded, (first, zero_index), (WIN * S_DEV, 2 * DH))
        new_part = old_part + jnp.concatenate([key_part, value_part], axis=1)
        grads_padded = lax.dynamic_update_slice(grads_padded, new_part, (first, zero_index))
        return grads_padded, (attended.reshape(S_DEV, HQ * DH), query_grad.reshape(S_DEV, HQ * DH))

    start_grads = jnp.zeros((margin + TOKENS, 2 * DH), jnp.float32)
    grads_padded, outputs = lax.scan(block_step, start_grads, jnp.arange(N_SEQ, dtype=jnp.int32))
    attended = outputs[0].reshape(TOKENS, HQ * DH)
    query_grad = outputs[1].reshape(TOKENS, HQ * DH)
    key_grad = grads_padded[margin:, :DH].astype(jnp.bfloat16)
    value_grad = grads_padded[margin:, DH:].astype(jnp.bfloat16)
    return (attended, query_grad, key_grad, value_grad)
```

```python
import functools
import math

import jax
import jax.numpy as jnp
from jax import lax
from jax.experimental import pallas as pl
from jax.experimental.pallas import tpu as pltpu
from jax.sharding import PartitionSpec as P

MESH = pl.DeviceIdType.MESH
HIDDEN = -1e30
CHUNK = 256
EARLY = (0, 2, 1, 4, 3)
LATE = (6, 5, 7)
BACK = (7, 5, 3, 1, 6, 4, 2, 0)


def dot(left, right):
    return jnp.dot(left, right, preferred_element_type=jnp.float32)


def kernel(
    q_hbm, k_hbm, v_hbm, g_hbm, docs_hbm, att_hbm, dq_hbm, dk_hbm, dv_hbm,
    kbuf, vbuf, q_rows, g_rows, q_t, g_t, k_t, v_t, s_ref, dp_ref, p_bf, ds_bf, o_t,
    att, dq, part_v, part_k, send_v, send_k, mate_v, mate_k, far_v, far_k, out_k, out_v, docs,
    load_sem, store_sem, ks_sem, kr_sem, vs_sem, vr_sem, gs_sem, gr_sem, hs_sem, hr_sem,
):
    me, head = lax.axis_index("seq"), lax.axis_index("head")
    count = lax.axis_size("seq")
    odd = lax.rem(me, 2)
    mate = me + 1 - 2 * odd
    cross = lax.rem(me - 3 + 6 * odd + count, count)
    rows, width = k_hbm.shape
    heads = q_hbm.shape[1] // width
    total = rows * heads
    chunks = [slice(at, at + CHUNK) for at in range(0, total, CHUNK)]

    def away(steps):
        return lax.rem(me + steps + count, count)

    def remote(src, dst, send_sem, recv_sem, device):
        return pltpu.make_async_remote_copy(
            src_ref=src, dst_ref=dst, send_sem=send_sem, recv_sem=recv_sem,
            device_id=(device, head), device_id_type=MESH,
        )

    barrier = pltpu.get_barrier_semaphore()
    peers = [away(-4), away(4), cross, away(-2), away(2), mate]
    for peer in peers:
        pl.semaphore_signal(barrier, inc=1, device_id=(peer, head), device_id_type=MESH)

    def load(src, dst, at):
        copy = pltpu.make_async_copy(src, dst, load_sem.at[at])
        copy.start()
        return copy

    load_k = load(k_hbm, kbuf.at[0], 0)
    load_v = load(v_hbm, vbuf.at[0], 1)
    load_docs = load(docs_hbm, docs, 2)
    spans = [pl.ds(h * width, width) for h in range(heads)]
    tiles = [pl.ds(h * rows, rows) for h in range(heads)]
    load_q = [load(q_hbm.at[:, spans[h]], q_rows.at[tiles[h]], 3 + h) for h in range(heads)]
    load_g = [load(g_hbm.at[:, spans[h]], g_rows.at[tiles[h]], 3 + heads + h) for h in range(heads)]
    load_k.wait()
    load_v.wait()
    pl.semaphore_wait(barrier, len(peers))

    class Forward:
        def __init__(self, buf, send_sem, recv_sem):
            self.buf, self.send_sem, self.recv_sem, self.sent = buf, send_sem, recv_sem, []

        def push(self, slot, to_slot, device, at):
            copy = remote(
                self.buf.at[slot], self.buf.at[to_slot], self.send_sem.at[at],
                self.recv_sem.at[to_slot], device,
            )
            copy.start()
            return copy

        def wait(self, slot):
            remote(
                self.buf.at[slot], self.buf.at[slot], self.send_sem.at[0], self.recv_sem.at[slot], mate
            ).wait_recv()

        def own(self):
            self.sent.append(self.push(0, 4, away(4), 0))
            self.sent.append(self.push(0, 2, away(2), 1))

            @pl.when(odd == 0)
            def _():
                self.push(0, 1, mate, 6)

        def to_mate(self, slot, at):
            self.sent.append(self.push(slot, slot + 1 - 2 * odd, mate, at))

        def got2(self):
            self.wait(2)
            self.to_mate(2, 2)

        def got4(self):
            self.wait(4)
            self.sent.append(self.push(4, 6, away(2), 3))

            @pl.when(odd == 1)
            def _():
                self.push(4, 7, cross, 6)

            self.to_mate(4, 4)

        def got6(self):
            self.wait(6)
            self.to_mate(6, 5)

        def finish(self):
            for copy in self.sent:
                copy.wait_send()
            remote(
                self.buf.at[0], self.buf.at[1], self.send_sem.at[6], self.recv_sem.at[1], mate
            ).wait_send()

    class Back:
        def __init__(self, part, send, mates, far, send_sem, recv_sem, out):
            self.part, self.send, self.mates, self.far = part, send, mates, far
            self.send_sem, self.recv_sem, self.out, self.sent = send_sem, recv_sem, out, []

        def push(self, slot, dst, recv_at, device):
            copy = remote(
                self.send.at[slot], dst, self.send_sem.at[slot], self.recv_sem.at[recv_at], device
            )
            copy.start()
            self.sent.append(copy)

        def wait(self, dst, recv_at):
            remote(
                self.send.at[0], dst, self.send_sem.at[0], self.recv_sem.at[recv_at], mate
            ).wait_recv()

        def wait_mate(self, slot):
            self.wait(self.mates.at[slot], slot)
            return self.mates[slot].astype(jnp.float32)

        def wait_far(self, slot):
            self.wait(self.far.at[slot], 9 + slot)
            return self.far[slot].astype(jnp.float32)

        def give(self, d, value):
            if d % 2 == 0:
                self.part[d] = value
                return
            self.send[d] = value.astype(jnp.bfloat16)
            device = jnp.where(odd == 0, cross, mate) if d == 7 else mate
            slot = d + 1 - 2 * odd
            self.push(d, self.mates.at[slot], slot, device)

        def relay6(self):
            self.send[6] = (self.part[6] + self.wait_mate(6)).astype(jnp.bfloat16)
            self.push(6, self.far.at[0], 9, away(-2))

        def relay2(self):
            self.send[2] = (self.part[2] + self.wait_mate(2)).astype(jnp.bfloat16)
            self.push(2, self.far.at[2], 11, away(-2))

        def relay4(self):
            self.part[4] = self.part[4] + self.wait_mate(4) + self.wait_far(0)

            @pl.when(odd == 1)
            def _():
                self.part[4] = self.part[4] + self.wait_mate(8)

            self.send[4] = self.part[4].astype(jnp.bfloat16)
            self.push(4, self.far.at[1], 10, away(-4))

        def final(self):
            self.part[0] = self.part[0] + self.wait_far(2) + self.wait_far(1)

            @pl.when(odd == 0)
            def _():
                self.part[0] = self.part[0] + self.wait_mate(0)

            self.out[...] = self.part[0].astype(jnp.bfloat16)

        def finish(self):
            for copy in self.sent:
                copy.wait_send()

    keys = Forward(kbuf, ks_sem, kr_sem)
    values = Forward(vbuf, vs_sem, vr_sem)
    back_v = Back(part_v, send_v, mate_v, far_v, gs_sem, gr_sem, out_v)
    back_k = Back(part_k, send_k, mate_k, far_k, hs_sem, hr_sem, out_k)
    keys.own()
    values.own()

    load_docs.wait()
    end, start = jnp.int32(0), jnp.int32(0)
    for at in range(docs.shape[0]):
        end = end + docs[at]
        start = jnp.where(end <= me, end, start)
    reach = me - start
    hidden = [jnp.where(d <= reach, 0.0, HIDDEN).astype(jnp.float32) for d in range(8)]

    for h in range(heads):
        load_q[h].wait()
        q_t[:, spans[h]] = q_rows[tiles[h]].T

    score_scale = width ** (-0.5)
    rate = score_scale * math.log2(math.e)
    causal = lax.broadcasted_iota(jnp.int32, (rows, CHUNK), 0) <= (
        lax.broadcasted_iota(jnp.int32, (rows, CHUNK), 1) % rows
    )

    def score(d, tops):
        out = []
        for at, cols in enumerate(chunks):
            scores = dot(kbuf[d], q_t[:, cols])
            if d == 0:
                scores = jnp.where(causal, scores, HIDDEN)
            s_ref[d, :, cols] = scores
            top = jnp.max(scores, axis=0, keepdims=True) + hidden[d]
            out.append(top if tops is None else jnp.maximum(tops[at], top))
        k_t[:, d * rows : (d + 1) * rows] = kbuf[d].T
        return out

    def lift(d, tops, sums):
        out = []
        for at, cols in enumerate(chunks):
            raised = jnp.exp2(s_ref[d, :, cols] * rate - (tops[at] * rate - hidden[d]))
            s_ref[d, :, cols] = raised
            part = jnp.sum(raised, axis=0, keepdims=True)
            out.append(part if sums is None else sums[at] + part)
        return out

    tops = score(0, None)
    for h in range(heads):
        load_g[h].wait()
        g_t[:, spans[h]] = g_rows[tiles[h]].T
    v_t[:, 0:rows] = vbuf[0].T

    keys.got2()
    keys.got4()
    tops = score(2, tops)
    tops = score(4, tops)
    values.got2()
    keys.wait(1)
    tops = score(1, tops)
    keys.wait(3)
    tops = score(3, tops)
    values.got4()
    sums = None
    for d in EARLY:
        sums = lift(d, tops, sums)
    keys.got6()
    late = score(6, tops)
    keys.wait(7)
    late = score(7, late)
    keys.wait(5)
    late = score(5, late)
    late_sums = None
    for d in LATE:
        late_sums = lift(d, late, late_sums)
    early_norm, late_norm = [], []
    for at in range(len(chunks)):
        fade = jnp.exp2((tops[at] - late[at]) * rate)
        norm = 1.0 / (sums[at] * fade + late_sums[at])
        early_norm.append(fade * norm)
        late_norm.append(norm)

    for d in BACK:
        for at, cols in enumerate(chunks):
            norm = late_norm[at] if d in LATE else early_norm[at]
            weights = s_ref[d, :, cols] * norm
            s_ref[d, :, cols] = weights
            p_bf[d * rows : (d + 1) * rows, cols] = weights.astype(jnp.bfloat16)
        back_v.give(d, dot(p_bf[d * rows : (d + 1) * rows, :], g_rows[...]))

    def value_tile(d):
        v_t[:, d * rows : (d + 1) * rows] = vbuf[d].T
        for cols in chunks:
            dp_ref[d, :, cols] = dot(vbuf[d], g_t[:, cols])

    values.got6()
    for d in (0, 2, 4, 6):
        value_tile(d)
    back_v.relay6()
    for d in (1, 3, 7):
        values.wait(d)
        value_tile(d)
    back_v.relay2()
    values.wait(5)
    value_tile(5)
    back_v.relay4()

    deltas = []
    for cols in chunks:
        rounded = dot(v_t[...], p_bf[:, cols]).astype(jnp.bfloat16).astype(jnp.float32)
        o_t[:, cols] = rounded
        deltas.append(jnp.sum(rounded * g_t[:, cols].astype(jnp.float32), axis=0, keepdims=True))

    for d in BACK:
        for at, cols in enumerate(chunks):
            change = s_ref[d, :, cols] * (dp_ref[d, :, cols] - deltas[at]) * score_scale
            ds_bf[d * rows : (d + 1) * rows, cols] = change.astype(jnp.bfloat16)
        back_k.give(d, dot(ds_bf[d * rows : (d + 1) * rows, :], q_rows[...]))

    def store(src, dst, at):
        copy = pltpu.make_async_copy(src, dst, store_sem.at[at])
        copy.start()
        return copy

    for h in range(heads):
        att[:, spans[h]] = o_t[:, h * rows : (h + 1) * rows].T.astype(jnp.bfloat16)
    stores = [store(att, att_hbm, 0)]
    back_k.relay6()
    back_k.relay2()
    for cols in chunks:
        grads = dot(k_t[...], ds_bf[:, cols])
        for at in range(CHUNK // rows):
            h = cols.start // rows + at
            dq[:, spans[h]] = grads[:, at * rows : (at + 1) * rows].T.astype(jnp.bfloat16)
    stores.append(store(dq, dq_hbm, 1))
    back_k.relay4()
    back_v.final()
    stores.append(store(out_v, dv_hbm, 2))
    back_k.final()
    stores.append(store(out_k, dk_hbm, 3))
    for part in (keys, values, back_v, back_k):
        part.finish()
    for copy in stores:
        copy.wait()


def local(queries, key_rows, value_rows, out_grad, doc_blocks):
    rows, width = key_rows.shape
    heads = queries.shape[1] // width
    total = rows * heads
    span = 8 * rows
    bf, f32 = jnp.bfloat16, jnp.float32
    blocks = pltpu.VMEM((8, rows, width), bf)
    dma = pltpu.SemaphoreType.DMA
    anywhere = pl.BlockSpec(memory_space=pl.ANY)
    scratch = [
        blocks, blocks,
        pltpu.VMEM((total, width), bf), pltpu.VMEM((total, width), bf),
        pltpu.VMEM((width, total), bf), pltpu.VMEM((width, total), bf),
        pltpu.VMEM((width, span), bf), pltpu.VMEM((width, span), bf),
        pltpu.VMEM((8, rows, total), f32), pltpu.VMEM((8, rows, total), f32),
        pltpu.VMEM((span, total), bf), pltpu.VMEM((span, total), bf),
        pltpu.VMEM((width, total), f32),
        pltpu.VMEM((rows, heads * width), bf), pltpu.VMEM((rows, heads * width), bf),
        pltpu.VMEM((8, rows, width), f32), pltpu.VMEM((8, rows, width), f32),
        blocks, blocks,
        pltpu.VMEM((9, rows, width), bf), pltpu.VMEM((9, rows, width), bf),
        pltpu.VMEM((3, rows, width), bf), pltpu.VMEM((3, rows, width), bf),
        pltpu.VMEM((rows, width), bf), pltpu.VMEM((rows, width), bf),
        pltpu.SMEM(doc_blocks.shape, jnp.int32),
        dma((3 + 2 * heads,)), dma((4,)),
        dma((7,)), dma((8,)), dma((7,)), dma((8,)),
        dma((8,)), dma((12,)), dma((8,)), dma((12,)),
    ]
    return pl.pallas_call(
        kernel,
        out_shape=(
            jax.ShapeDtypeStruct(queries.shape, bf),
            jax.ShapeDtypeStruct(queries.shape, bf),
            jax.ShapeDtypeStruct(key_rows.shape, bf),
            jax.ShapeDtypeStruct(key_rows.shape, bf),
        ),
        in_specs=[anywhere] * 5,
        out_specs=(anywhere,) * 4,
        scratch_shapes=scratch,
        name="packed_attention",
        compiler_params=pltpu.CompilerParams(collective_id=0, has_side_effects=True),
    )(queries, key_rows, value_rows, out_grad, doc_blocks)


def solution(mesh):
    in_specs = (P("seq", "head"), P("seq", "head"), P("seq", "head"), P("seq", "head"), P())
    out_specs = (P("seq", "head"), P("seq", "head"), P("seq", "head"), P("seq", "head"))
    return jax.shard_map(local, mesh=mesh, in_specs=in_specs, out_specs=out_specs, check_vma=False)
```

```python
import functools
import math

import jax
import jax.numpy as jnp
from jax import lax
from jax.experimental import pallas as pl
from jax.experimental.pallas import tpu as pltpu
from jax.sharding import PartitionSpec as P

MESH = pl.DeviceIdType.MESH
HIDDEN = -1e30
CHUNK = 256
SLOTS = 8
BACK = (7, 5, 3, 1, 6, 4, 2, 0)


def dot(left, right):
    return jnp.dot(left, right, preferred_element_type=jnp.float32)


def kernel(
    q_hbm, k_hbm, v_hbm, g_hbm, docs_hbm, att_out, dq_out, dk_out, dv_out,
    kbuf, vbuf, q_rows, g_rows, q_t, g_t, k_t, v_t, s_ref, dp_ref, p_bf, ds_bf, o_t,
    att, dq, part_v, part_k, send_v, send_k, mate_v, mate_k, far_v, far_k, out_k, out_v, docs,
    load_sem, store_sem, ks_sem, kr_sem, vs_sem, vr_sem, gs_sem, gm_sem, gf_sem, hs_sem, hm_sem, hf_sem,
):
    me, head = lax.axis_index("seq"), lax.axis_index("head")
    final_device = lax.axis_size("seq") - 1
    odd = lax.rem(me, 2)
    even = odd == 0
    mate = me + 1 - 2 * odd
    rows, width = k_hbm.shape
    heads = q_hbm.shape[1] // width
    total = rows * heads
    chunks = [slice(at, at + CHUNK) for at in range(0, total, CHUNK)]
    last = jnp.where((me >= 1) & (me < SLOTS), me, SLOTS - 1)

    def remote(src, dst, send_sem, recv_sem, device):
        return pltpu.make_async_remote_copy(
            src_ref=src, dst_ref=dst, send_sem=send_sem, recv_sem=recv_sem,
            device_id=(device, head), device_id_type=MESH,
        )

    barrier = pltpu.get_barrier_semaphore()

    def greet(when, device):
        @pl.when(when)
        def _():
            pl.semaphore_signal(barrier, inc=1, device_id=(device, head), device_id_type=MESH)

    greet(me >= 6, jnp.where(me < 8, 0, me - 4))
    greet((me >= 4) & (me < 8), me - 4)
    greet((me >= 8) & even, me - 3)
    greet(me >= 2, me - 2)
    greet((odd == 1) | (me >= 2), mate)

    def load(src, dst, at):
        copy = pltpu.make_async_copy(src, dst, load_sem.at[at])
        copy.start()
        return copy

    load_k = load(k_hbm, kbuf.at[0], 0)
    load_v = load(v_hbm, vbuf.at[0], 1)
    load_docs = load(docs_hbm, docs, 2)
    spans = [pl.ds(h * width, width) for h in range(heads)]
    tiles = [pl.ds(h * rows, rows) for h in range(heads)]
    load_q = [load(q_hbm.at[:, spans[h]], q_rows.at[tiles[h]], 3 + h) for h in range(heads)]
    load_g = [load(g_hbm.at[:, spans[h]], g_rows.at[tiles[h]], 3 + heads + h) for h in range(heads)]

    def yes(condition):
        return jnp.where(condition, 1, 0)

    pl.semaphore_wait(
        barrier,
        yes(me + 2 <= final_device) + yes(me + 4 <= final_device) + yes(even | (me >= 3))
        + yes((odd == 1) & (me >= 5) & (me + 3 <= final_device)) + 2 * yes(me == 0),
    )

    class Forward:
        def __init__(self, block, buf, send_sem, recv_sem):
            self.block, self.buf, self.send_sem, self.recv_sem = block, buf, send_sem, recv_sem
            self.sent = []

        def push(self, when, slot, to_slot, device, at):
            src = self.block if isinstance(slot, int) and slot == 0 else self.buf.at[slot]

            @pl.when(when)
            def _():
                remote(
                    src, self.buf.at[to_slot], self.send_sem.at[at], self.recv_sem.at[to_slot], device
                ).start()

            self.sent.append((when, at))

        def wait(self, slot, when=True):
            @pl.when((me >= slot) & when)
            def _():
                remote(
                    self.buf.at[slot], self.buf.at[slot], self.send_sem.at[0], self.recv_sem.at[slot], mate
                ).wait_recv()

        def far(self):
            self.push(me == 0, 0, 7, 7, 7)
            self.push(me == 0, 0, 6, 6, 8)

        def near(self):
            self.push(me + 4 <= final_device, 0, 4, me + 4, 0)
            self.push(even, 0, 1, mate, 6)
            self.push(me + 2 <= final_device, 0, 2, me + 2, 1)

        def across(self, slot, at, when):
            self.push((me >= slot) & when, slot, slot + 1 - 2 * odd, mate, at)

        def got(self, slot):
            ready = last != slot

            @pl.when(ready)
            def _():
                self.wait(slot)

            if slot == 4:
                self.push((me >= 5) & (me + 2 <= final_device), 4, 6, me + 2, 3)
                self.push((me >= 5) & (odd == 1) & (me + 3 <= final_device), 4, 7, me + 3, 9)
            self.across(slot, slot // 2 + 1 if slot < 6 else 5, ready)

        def got_last(self):
            self.wait(last)
            self.push((me == 2) | (me == 4), last, last + 1, mate, 10)

        def finish(self):
            for when, at in self.sent:
                @pl.when(when)
                def _():
                    remote(
                        self.buf.at[0], self.buf.at[1], self.send_sem.at[at], self.recv_sem.at[1], mate
                    ).wait_send()

    class Back:
        def __init__(self, part, send, mates, far, send_sem, mate_sem, far_sem, out):
            self.part, self.send, self.mates, self.far, self.out = part, send, mates, far, out
            self.send_sem, self.mate_sem, self.far_sem = send_sem, mate_sem, far_sem
            self.sent = []

        def push(self, when, d, dst, recv_sem, device):
            @pl.when(when)
            def _():
                remote(self.send.at[d], dst, self.send_sem.at[d], recv_sem, device).start()

        def give(self, d):
            slot = d + 1 - 2 * odd
            if d == 7:
                self.push((me >= d) & even, d, self.far.at[3], self.far_sem.at[3], me - d)
                self.push((me >= d) & (odd == 1), d, self.mates.at[6], self.mate_sem.at[6], mate)
            else:
                self.push(me >= d, d, self.mates.at[slot], self.mate_sem.at[slot], mate)
            self.sent.append(d)

        def wait_mate(self, slot):
            remote(
                self.send.at[0], self.mates.at[slot], self.send_sem.at[0], self.mate_sem.at[slot], mate
            ).wait_recv()
            return self.mates[slot].astype(jnp.float32)

        def wait_far(self, at):
            remote(
                self.send.at[0], self.far.at[at], self.send_sem.at[0], self.far_sem.at[at], mate
            ).wait_recv()
            return self.far[at].astype(jnp.float32)

        def relay(self, d):
            @pl.when(me >= d)
            def _():
                self.send[d] = (self.part[d] + self.wait_mate(d)).astype(jnp.bfloat16)
                at = d // 2 - 1
                remote(
                    self.send.at[d], self.far.at[at], self.send_sem.at[d], self.far_sem.at[at], me - d
                ).start()

            self.sent.append(d)

        def final(self):
            @pl.when(even)
            def _():
                self.part[0] = self.part[0] + self.wait_mate(0)

            for at, steps in ((0, 2), (1, 4), (2, 6)):
                @pl.when(me + steps <= final_device)
                def _():
                    self.part[0] = self.part[0] + self.wait_far(at)

            @pl.when((odd == 1) & (me + 7 <= final_device))
            def _():
                self.part[0] = self.part[0] + self.wait_far(3)

            self.out[...] = self.part[0].astype(jnp.bfloat16)

        def finish(self):
            for d in self.sent:
                @pl.when(me >= d)
                def _():
                    remote(
                        self.send.at[d], self.far.at[0], self.send_sem.at[d], self.far_sem.at[0], mate
                    ).wait_send()

    keys = Forward(k_hbm, kbuf, ks_sem, kr_sem)
    values = Forward(v_hbm, vbuf, vs_sem, vr_sem)
    back_v = Back(part_v, send_v, mate_v, far_v, gs_sem, gm_sem, gf_sem, out_v)
    back_k = Back(part_k, send_k, mate_k, far_k, hs_sem, hm_sem, hf_sem, out_k)
    keys.far()
    values.far()
    keys.near()
    values.near()

    for d in range(1, SLOTS):
        @pl.when(me < d)
        def _():
            kbuf[d] = jnp.zeros_like(kbuf[d])
            vbuf[d] = jnp.zeros_like(vbuf[d])

    load_docs.wait()
    end, start = jnp.int32(0), jnp.int32(0)
    for at in range(docs.shape[0]):
        end = end + docs[at]
        start = jnp.where(end <= me, end, start)
    reach = me - start

    def place(d):
        at = jnp.where(lax.rem(d, 2) == 1, (SLOTS - 1 - d) // 2, SLOTS - 1 - d // 2)
        return pl.ds(pl.multiple_of(at * rows, rows), rows)

    score_scale = width ** (-0.5)
    rate = score_scale * math.log2(math.e)
    causal = lax.broadcasted_iota(jnp.int32, (rows, CHUNK), 0) <= (
        lax.broadcasted_iota(jnp.int32, (rows, CHUNK), 1) % rows
    )

    def hidden(d):
        return jnp.where(d <= reach, 0.0, HIDDEN).astype(jnp.float32)

    def score(d, tops, own=False):
        out = []
        block = kbuf[d]
        for at, cols in enumerate(chunks):
            scores = dot(block, q_t[:, cols])
            if own:
                scores = jnp.where(causal, scores, HIDDEN)
            s_ref[d, :, cols] = scores
            top = jnp.max(scores, axis=0, keepdims=True) + hidden(d)
            out.append(top if tops is None else jnp.maximum(tops[at], top))
        k_t[:, place(d)] = block.T
        return out

    def lift(d, tops, sums):
        out = []
        for at, cols in enumerate(chunks):
            raised = jnp.exp2(s_ref[d, :, cols] * rate - (tops[at] * rate - hidden(d)))
            s_ref[d, :, cols] = raised
            part = jnp.sum(raised, axis=0, keepdims=True)
            out.append(part if sums is None else sums[at] + part)
        return out

    def value_tile(d):
        block = vbuf[d]
        v_t[:, place(d)] = block.T
        for cols in chunks:
            dp_ref[d, :, cols] = dot(block, g_t[:, cols])

    early = [jnp.int32(0)] + [j + yes(j >= last) for j in range(1, SLOTS - 1)]

    for h in range(heads):
        load_q[h].wait()
        q_t[:, spans[h]] = q_rows[tiles[h]].T
    keys.got(2)
    load_k.wait()
    tops = score(early[0], None, own=True)
    keys.got(4)
    values.got(2)
    for h in range(heads):
        load_g[h].wait()
        g_t[:, spans[h]] = g_rows[tiles[h]].T
    load_v.wait()
    values.got(4)
    value_tile(early[0])
    keys.got(6)
    for d in early[1:4]:
        keys.wait(d, lax.rem(d, 2) == 1)
        tops = score(d, tops)
    values.got(6)
    for d in early[4:]:
        keys.wait(d, lax.rem(d, 2) == 1)
        tops = score(d, tops)
    sums = None
    for d in early:
        sums = lift(d, tops, sums)
    for d in early[1:]:
        values.wait(d, lax.rem(d, 2) == 1)
        value_tile(d)

    keys.got_last()
    late = score(last, tops)
    late_sums = lift(last, late, None)
    values.got_last()
    value_tile(last)
    early_norm, late_norm = [], []
    for at in range(len(chunks)):
        fade = jnp.exp2((tops[at] - late[at]) * rate)
        norm = 1.0 / (sums[at] * fade + late_sums[at])
        early_norm.append(fade * norm)
        late_norm.append(norm)

    half = SLOTS // 2
    groups = (BACK[:half], BACK[half:])

    def deliver(back, group, grads):
        for at, d in enumerate(group):
            tile = grads[at * rows : (at + 1) * rows]
            if d % 2 == 1:
                back.send[d] = tile.astype(jnp.bfloat16)
                back.give(d)
            else:
                back.part[d] = tile

    def norms(d, at):
        return jnp.where(d == last, late_norm[at], early_norm[at]) if d else early_norm[at]

    for number, group in enumerate(groups):
        base = number * half * rows
        for at, d in enumerate(group):
            for c, cols in enumerate(chunks):
                weights = s_ref[d, :, cols] * norms(d, c)
                p_bf[base + at * rows : base + (at + 1) * rows, cols] = weights.astype(jnp.bfloat16)
        deliver(back_v, group, dot(p_bf[base : base + half * rows, :], g_rows[...]))

    deltas = []
    for cols in chunks:
        rounded = dot(v_t[...], p_bf[:, cols]).astype(jnp.bfloat16).astype(jnp.float32)
        o_t[:, cols] = rounded
        deltas.append(jnp.sum(rounded * g_t[:, cols].astype(jnp.float32), axis=0, keepdims=True))

    for number, group in enumerate(groups):
        base = number * half * rows
        for at, d in enumerate(group):
            for c, cols in enumerate(chunks):
                change = s_ref[d, :, cols] * ((dp_ref[d, :, cols] - deltas[c]) * (norms(d, c) * score_scale))
                ds_bf[base + at * rows : base + (at + 1) * rows, cols] = change.astype(jnp.bfloat16)
        deliver(back_k, group, dot(ds_bf[base : base + half * rows, :], q_rows[...]))

    def store(src, dst, at):
        copy = pltpu.make_async_copy(src, dst, store_sem.at[at])
        copy.start()
        return copy

    for d in (6, 4, 2):
        back_k.relay(d)
    for d in (6, 4, 2):
        back_v.relay(d)
    for h in range(heads):
        att[:, spans[h]] = o_t[:, h * rows : (h + 1) * rows].T.astype(jnp.bfloat16)
    stores = [store(att, att_out, 0)]
    for cols in chunks:
        grads = dot(k_t[...], ds_bf[:, cols])
        for at in range(CHUNK // rows):
            h = cols.start // rows + at
            dq[:, spans[h]] = grads[:, at * rows : (at + 1) * rows].T.astype(jnp.bfloat16)
    stores.append(store(dq, dq_out, 1))
    back_v.final()
    stores.append(store(out_v, dv_out, 2))
    back_k.final()
    stores.append(store(out_k, dk_out, 3))
    for part in (keys, values, back_v, back_k):
        part.finish()
    for copy in stores:
        copy.wait()


def hand_on(*refs):
    sources, results, staged, sems = refs[:4], refs[4:8], refs[8:12], refs[12]
    pieces = []
    for source, result, stage in zip(sources, results, staged):
        half = source.shape[0] // 2
        for at in (pl.ds(0, half), pl.ds(half, half)):
            pieces.append((source.at[at], stage.at[at], result.at[at]))
    reads = [pltpu.make_async_copy(p[0], p[1], sems.at[0, at]) for at, p in enumerate(pieces)]
    writes = [pltpu.make_async_copy(p[1], p[2], sems.at[1, at]) for at, p in enumerate(pieces)]
    for read in reads:
        read.start()
    for read, write in zip(reads, writes):
        read.wait()
        write.start()
    for write in writes:
        write.wait()


def local(queries, key_rows, value_rows, out_grad, doc_blocks):
    rows, width = key_rows.shape
    heads = queries.shape[1] // width
    total = rows * heads
    span = SLOTS * rows
    bf, f32 = jnp.bfloat16, jnp.float32
    blocks = pltpu.VMEM((SLOTS, rows, width), bf)
    dma = pltpu.SemaphoreType.DMA
    anywhere = pl.BlockSpec(memory_space=pl.ANY)
    scratch = [
        blocks, blocks,
        pltpu.VMEM((total, width), bf), pltpu.VMEM((total, width), bf),
        pltpu.VMEM((width, total), bf), pltpu.VMEM((width, total), bf),
        pltpu.VMEM((width, span), bf), pltpu.VMEM((width, span), bf),
        pltpu.VMEM((SLOTS, rows, total), f32), pltpu.VMEM((SLOTS, rows, total), f32),
        pltpu.VMEM((span, total), bf), pltpu.VMEM((span, total), bf),
        pltpu.VMEM((width, total), f32),
        pltpu.VMEM((rows, heads * width), bf), pltpu.VMEM((rows, heads * width), bf),
        pltpu.VMEM((SLOTS, rows, width), f32), pltpu.VMEM((SLOTS, rows, width), f32),
        blocks, blocks,
        blocks, blocks,
        pltpu.VMEM((4, rows, width), bf), pltpu.VMEM((4, rows, width), bf),
        pltpu.VMEM((rows, width), bf), pltpu.VMEM((rows, width), bf),
        pltpu.SMEM(doc_blocks.shape, jnp.int32),
        dma((3 + 2 * heads,)), dma((4,)),
        dma((11,)), dma((8,)), dma((11,)), dma((8,)),
        dma((8,)), dma((8,)), dma((4,)), dma((8,)), dma((8,)), dma((4,)),
    ]
    results = (
        jax.ShapeDtypeStruct(queries.shape, bf),
        jax.ShapeDtypeStruct(queries.shape, bf),
        jax.ShapeDtypeStruct(key_rows.shape, bf),
        jax.ShapeDtypeStruct(key_rows.shape, bf),
    )
    outputs = pl.pallas_call(
        kernel,
        out_shape=results,
        in_specs=[pl.BlockSpec(memory_space=pltpu.HBM)] * 4 + [anywhere],
        out_specs=(anywhere,) * 4,
        scratch_shapes=scratch,
        name="packed_attention",
        compiler_params=pltpu.CompilerParams(
            collective_id=0, has_side_effects=True
        ),
    )(queries, key_rows, value_rows, out_grad, doc_blocks)
    return pl.pallas_call(
        hand_on,
        out_shape=results,
        in_specs=[anywhere] * 4,
        out_specs=(anywhere,) * 4,
        scratch_shapes=[pltpu.VMEM(r.shape, r.dtype) for r in results] + [dma((2, 8))],
        name="hand_on",
    )(*outputs)


def solution(mesh):
    in_specs = (P("seq", "head"), P("seq", "head"), P("seq", "head"), P("seq", "head"), P())
    out_specs = (P("seq", "head"), P("seq", "head"), P("seq", "head"), P("seq", "head"))
    return jax.shard_map(local, mesh=mesh, in_specs=in_specs, out_specs=out_specs, check_vma=False)
```

```python
import functools
import math

import jax
import jax.numpy as jnp
from jax import lax
from jax.experimental import pallas as pl
from jax.experimental.pallas import tpu as pltpu
from jax.sharding import PartitionSpec as P

MESH = pl.DeviceIdType.MESH
HIDDEN = -1e30
CHUNK = 256
SLOTS = 8
BACK = (7, 5, 3, 1, 6, 4, 2, 0)


def dot(left, right):
    return jnp.dot(left, right, preferred_element_type=jnp.float32)


def kernel(
    q_hbm, k_hbm, v_hbm, g_hbm, docs_hbm, att_out, dq_out, dk_out, dv_out,
    kbuf, vbuf, q_rows, g_rows, q_t, g_t, k_t, v_t, s_ref, dp_ref, p_bf, ds_bf, o_t,
    att, dq, part_v, part_k, send_v, send_k, mate_v, mate_k, far_v, far_k, out_k, out_v, docs,
    load_sem, store_sem, ks_sem, kr_sem, vs_sem, vr_sem, gs_sem, gm_sem, gf_sem, hs_sem, hm_sem, hf_sem,
):
    me, head = lax.axis_index("seq"), lax.axis_index("head")
    final_device = lax.axis_size("seq") - 1
    odd = lax.rem(me, 2)
    even = odd == 0
    mate = me + 1 - 2 * odd
    rows, width = k_hbm.shape
    heads = q_hbm.shape[1] // width
    total = rows * heads
    chunks = [slice(at, at + CHUNK) for at in range(0, total, CHUNK)]
    last = jnp.where((me >= 1) & (me < SLOTS), me, SLOTS - 1)

    def remote(src, dst, send_sem, recv_sem, device):
        return pltpu.make_async_remote_copy(
            src_ref=src, dst_ref=dst, send_sem=send_sem, recv_sem=recv_sem,
            device_id=(device, head), device_id_type=MESH,
        )

    barrier = pltpu.get_barrier_semaphore()

    def greet(when, device):
        @pl.when(when)
        def _():
            pl.semaphore_signal(barrier, inc=1, device_id=(device, head), device_id_type=MESH)

    greet(me >= 6, jnp.where(me < 8, 0, me - 4))
    greet((me >= 4) & (me < 8), me - 4)
    greet((me >= 8) & even, me - 3)
    greet(me >= 2, me - 2)
    greet((odd == 1) | (me >= 2), mate)

    def load(src, dst, at):
        copy = pltpu.make_async_copy(src, dst, load_sem.at[at])
        copy.start()
        return copy

    load_k = load(k_hbm, kbuf.at[0], 0)
    load_v = load(v_hbm, vbuf.at[0], 1)
    load_docs = load(docs_hbm, docs, 2)
    spans = [pl.ds(h * width, width) for h in range(heads)]
    tiles = [pl.ds(h * rows, rows) for h in range(heads)]
    load_q = [load(q_hbm.at[:, spans[h]], q_rows.at[tiles[h]], 3 + h) for h in range(heads)]
    load_g = [load(g_hbm.at[:, spans[h]], g_rows.at[tiles[h]], 3 + heads + h) for h in range(heads)]

    def yes(condition):
        return jnp.where(condition, 1, 0)

    pl.semaphore_wait(
        barrier,
        yes(me + 2 <= final_device) + yes(me + 4 <= final_device) + yes(even | (me >= 3))
        + yes((odd == 1) & (me >= 5) & (me + 3 <= final_device)) + 2 * yes(me == 0),
    )

    class Forward:
        def __init__(self, block, buf, send_sem, recv_sem):
            self.block, self.buf, self.send_sem, self.recv_sem = block, buf, send_sem, recv_sem
            self.sent = []

        def push(self, when, slot, to_slot, device, at):
            src = self.block if isinstance(slot, int) and slot == 0 else self.buf.at[slot]

            @pl.when(when)
            def _():
                remote(
                    src, self.buf.at[to_slot], self.send_sem.at[at], self.recv_sem.at[to_slot], device
                ).start()

            self.sent.append((when, at))

        def wait(self, slot, when=True):
            @pl.when((me >= slot) & when)
            def _():
                remote(
                    self.buf.at[slot], self.buf.at[slot], self.send_sem.at[0], self.recv_sem.at[slot], mate
                ).wait_recv()

        def far(self):
            self.push(me == 0, 0, 7, 7, 7)
            self.push(me == 0, 0, 6, 6, 8)

        def near(self):
            self.push(me + 4 <= final_device, 0, 4, me + 4, 0)
            self.push(even, 0, 1, mate, 6)
            self.push(me + 2 <= final_device, 0, 2, me + 2, 1)

        def across(self, slot, at, when):
            self.push((me >= slot) & when, slot, slot + 1 - 2 * odd, mate, at)

        def got(self, slot):
            ready = last != slot

            @pl.when(ready)
            def _():
                self.wait(slot)

            if slot == 4:
                self.push((me >= 5) & (me + 2 <= final_device), 4, 6, me + 2, 3)
                self.push((me >= 5) & (odd == 1) & (me + 3 <= final_device), 4, 7, me + 3, 9)
            self.across(slot, slot // 2 + 1 if slot < 6 else 5, ready)

        def got_last(self, when=True):
            self.wait(last, when)

        def last_across(self):
            self.push((me == 2) | (me == 4), last, last + 1, mate, 10)

        def finish(self):
            for when, at in self.sent:
                @pl.when(when)
                def _():
                    remote(
                        self.buf.at[0], self.buf.at[1], self.send_sem.at[at], self.recv_sem.at[1], mate
                    ).wait_send()

    class Back:
        def __init__(self, part, send, mates, far, send_sem, mate_sem, far_sem, out):
            self.part, self.send, self.mates, self.far, self.out = part, send, mates, far, out
            self.send_sem, self.mate_sem, self.far_sem = send_sem, mate_sem, far_sem
            self.sent = []

        def push(self, when, d, dst, recv_sem, device):
            @pl.when(when)
            def _():
                remote(self.send.at[d], dst, self.send_sem.at[d], recv_sem, device).start()

        def give(self, d):
            slot = d + 1 - 2 * odd
            if d == 7:
                self.push((me >= d) & even, d, self.far.at[3], self.far_sem.at[3], me - 3)
                self.push((me >= d) & (odd == 1), d, self.mates.at[6], self.mate_sem.at[6], mate)
            else:
                self.push(me >= d, d, self.mates.at[slot], self.mate_sem.at[slot], mate)
            self.sent.append(d)

        def wait_mate(self, slot):
            remote(
                self.send.at[0], self.mates.at[slot], self.send_sem.at[0], self.mate_sem.at[slot], mate
            ).wait_recv()
            return self.mates[slot].astype(jnp.float32)

        def wait_far(self, at):
            remote(
                self.send.at[0], self.far.at[at], self.send_sem.at[0], self.far_sem.at[at], mate
            ).wait_recv()
            return self.far[at].astype(jnp.float32)

        def relay(self, d, when=True):
            def send(at, device):
                remote(
                    self.send.at[d], self.far.at[at], self.send_sem.at[d], self.far_sem.at[at], device
                ).start()

            @pl.when((me >= d) & when)
            def _():
                self.part[d] = self.part[d] + self.wait_mate(d)
                if d == 4:
                    @pl.when((me >= 6) & (me + 2 <= final_device))
                    def _():
                        self.part[d] = self.part[d] + self.wait_far(4)

                    @pl.when((odd == 1) & (me >= 5) & (me + 3 <= final_device))
                    def _():
                        self.part[d] = self.part[d] + self.wait_far(3)

                self.send[d] = self.part[d].astype(jnp.bfloat16)
                if d == 6:
                    pl.when(me >= SLOTS)(lambda: send(4, me - 2))
                    pl.when(me < SLOTS)(lambda: send(2, me - 6))
                else:
                    send(d // 2 - 1, me - d)

            if d not in self.sent:
                self.sent.append(d)

        def final(self):
            @pl.when(even)
            def _():
                self.part[0] = self.part[0] + self.wait_mate(0)

            for at, steps, limit in ((0, 2, final_device), (1, 4, final_device), (2, 6, SLOTS - 1)):
                @pl.when(me + steps <= limit)
                def _():
                    self.part[0] = self.part[0] + self.wait_far(at)

            self.out[...] = self.part[0].astype(jnp.bfloat16)

        def finish(self):
            for d in self.sent:
                @pl.when(me >= d)
                def _():
                    remote(
                        self.send.at[d], self.far.at[0], self.send_sem.at[d], self.far_sem.at[0], mate
                    ).wait_send()

    keys = Forward(k_hbm, kbuf, ks_sem, kr_sem)
    values = Forward(v_hbm, vbuf, vs_sem, vr_sem)
    back_v = Back(part_v, send_v, mate_v, far_v, gs_sem, gm_sem, gf_sem, out_v)
    back_k = Back(part_k, send_k, mate_k, far_k, hs_sem, hm_sem, hf_sem, out_k)
    keys.far()
    values.far()
    keys.near()
    values.near()

    for d in range(1, SLOTS):
        @pl.when(me < d)
        def _():
            kbuf[d] = jnp.zeros_like(kbuf[d])
            vbuf[d] = jnp.zeros_like(vbuf[d])

    load_docs.wait()
    end, start = jnp.int32(0), jnp.int32(0)
    for at in range(docs.shape[0]):
        end = end + docs[at]
        start = jnp.where(end <= me, end, start)
    reach = me - start

    def place(d):
        at = jnp.where(lax.rem(d, 2) == 1, (SLOTS - 1 - d) // 2, SLOTS - 1 - d // 2)
        return pl.ds(pl.multiple_of(at * rows, rows), rows)

    score_scale = width ** (-0.5)
    rate = score_scale * math.log2(math.e)
    causal = lax.broadcasted_iota(jnp.int32, (rows, CHUNK), 0) <= (
        lax.broadcasted_iota(jnp.int32, (rows, CHUNK), 1) % rows
    )

    def hidden(d):
        return jnp.where(d <= reach, 0.0, HIDDEN).astype(jnp.float32)

    def score(d, tops, own=False):
        out = []
        block = kbuf[d]
        for at, cols in enumerate(chunks):
            scores = dot(block, q_t[:, cols])
            if own:
                scores = jnp.where(causal, scores, HIDDEN)
            s_ref[d, :, cols] = scores
            top = jnp.max(scores, axis=0, keepdims=True) + hidden(d)
            out.append(top if tops is None else jnp.maximum(tops[at], top))
        k_t[:, place(d)] = block.T
        return out

    def lift(d, tops, sums):
        out = []
        for at, cols in enumerate(chunks):
            raised = jnp.exp2(s_ref[d, :, cols] * rate - (tops[at] * rate - hidden(d)))
            s_ref[d, :, cols] = raised
            part = jnp.sum(raised, axis=0, keepdims=True)
            out.append(part if sums is None else sums[at] + part)
        return out

    def value_tile(d):
        block = vbuf[d]
        v_t[:, place(d)] = block.T
        for cols in chunks:
            dp_ref[d, :, cols] = dot(block, g_t[:, cols])

    early = [jnp.int32(0)] + [j + yes(j >= last) for j in range(1, SLOTS - 1)]

    for h in range(heads):
        load_q[h].wait()
        q_t[:, spans[h]] = q_rows[tiles[h]].T
    keys.got(2)
    load_k.wait()
    tops = score(early[0], None, own=True)
    keys.got(4)
    values.got(2)
    for h in range(heads):
        load_g[h].wait()
        g_t[:, spans[h]] = g_rows[tiles[h]].T
    load_v.wait()
    values.got(4)
    value_tile(early[0])
    keys.got(6)
    for d in early[1:4]:
        keys.wait(d, lax.rem(d, 2) == 1)
        tops = score(d, tops)
    values.got(6)
    for d in early[4:]:
        keys.wait(d, lax.rem(d, 2) == 1)
        tops = score(d, tops)
    sums = None
    for d in early:
        sums = lift(d, tops, sums)
    for d in early[1:4]:
        values.wait(d, lax.rem(d, 2) == 1)
        value_tile(d)

    passes_on = (me == 2) | (me == 4)
    outer = me < SLOTS
    keys.got_last()
    keys.last_across()
    late = score(last, tops)
    late_sums = lift(last, late, None)
    values.got_last(passes_on)
    values.last_across()
    early_norm, late_norm = [], []
    for at in range(len(chunks)):
        fade = jnp.exp2((tops[at] - late[at]) * rate)
        norm = 1.0 / (sums[at] * fade + late_sums[at])
        early_norm.append(fade * norm)
        late_norm.append(norm)

    half = SLOTS // 2
    groups = (BACK[:half], BACK[half:])

    def deliver(back, group, grads):
        for at, d in enumerate(group):
            tile = grads[at * rows : (at + 1) * rows]
            if d % 2 == 1:
                back.send[d] = tile.astype(jnp.bfloat16)
                back.give(d)
            else:
                back.part[d] = tile

    def norms(d, at):
        return jnp.where(d == last, late_norm[at], early_norm[at]) if d else early_norm[at]

    for number, group in enumerate(groups):
        base = number * half * rows
        for at, d in enumerate(group):
            for c, cols in enumerate(chunks):
                weights = s_ref[d, :, cols] * norms(d, c)
                p_bf[base + at * rows : base + (at + 1) * rows, cols] = weights.astype(jnp.bfloat16)
        deliver(back_v, group, dot(p_bf[base : base + half * rows, :], g_rows[...]))

    for d in early[4:]:
        values.wait(d, lax.rem(d, 2) == 1)
        value_tile(d)
    back_v.relay(6, me >= SLOTS)
    back_v.relay(2, me >= SLOTS)
    values.got_last(jnp.logical_not(passes_on))
    value_tile(last)

    deltas = []
    for cols in chunks:
        rounded = dot(v_t[...], p_bf[:, cols]).astype(jnp.bfloat16).astype(jnp.float32)
        o_t[:, cols] = rounded
        deltas.append(jnp.sum(rounded * g_t[:, cols].astype(jnp.float32), axis=0, keepdims=True))

    for number, group in enumerate(groups):
        base = number * half * rows
        for at, d in enumerate(group):
            for c, cols in enumerate(chunks):
                change = s_ref[d, :, cols] * ((dp_ref[d, :, cols] - deltas[c]) * (norms(d, c) * score_scale))
                ds_bf[base + at * rows : base + (at + 1) * rows, cols] = change.astype(jnp.bfloat16)
        deliver(back_k, group, dot(ds_bf[base : base + half * rows, :], q_rows[...]))

    def store(src, dst, at):
        copy = pltpu.make_async_copy(src, dst, store_sem.at[at])
        copy.start()
        return copy

    back_k.relay(6)
    back_v.relay(4, me >= SLOTS)
    for d in (4, 2):
        back_k.relay(d, outer)
    for d in (6, 4, 2):
        back_v.relay(d, outer)
    back_k.relay(2, me >= SLOTS)
    for h in range(heads):
        att[:, spans[h]] = o_t[:, h * rows : (h + 1) * rows].T.astype(jnp.bfloat16)
    stores = [store(att, att_out, 0)]
    for cols in chunks:
        grads = dot(k_t[...], ds_bf[:, cols])
        for at in range(CHUNK // rows):
            h = cols.start // rows + at
            dq[:, spans[h]] = grads[:, at * rows : (at + 1) * rows].T.astype(jnp.bfloat16)
    stores.append(store(dq, dq_out, 1))
    back_k.relay(4, me >= SLOTS)
    back_v.final()
    stores.append(store(out_v, dv_out, 2))
    back_k.final()
    stores.append(store(out_k, dk_out, 3))
    for part in (keys, values, back_v, back_k):
        part.finish()
    for copy in stores:
        copy.wait()


def hand_on(*refs):
    sources, results, staged, sems = refs[:4], refs[4:8], refs[8:12], refs[12]
    pieces = []
    for source, result, stage in zip(sources, results, staged):
        half = source.shape[0] // 2
        for at in (pl.ds(0, half), pl.ds(half, half)):
            pieces.append((source.at[at], stage.at[at], result.at[at]))
    reads = [pltpu.make_async_copy(p[0], p[1], sems.at[0, at]) for at, p in enumerate(pieces)]
    writes = [pltpu.make_async_copy(p[1], p[2], sems.at[1, at]) for at, p in enumerate(pieces)]
    for read in reads:
        read.start()
    for read, write in zip(reads, writes):
        read.wait()
        write.start()
    for write in writes:
        write.wait()


def local(queries, key_rows, value_rows, out_grad, doc_blocks):
    rows, width = key_rows.shape
    heads = queries.shape[1] // width
    total = rows * heads
    span = SLOTS * rows
    bf, f32 = jnp.bfloat16, jnp.float32
    blocks = pltpu.VMEM((SLOTS, rows, width), bf)
    dma = pltpu.SemaphoreType.DMA
    anywhere = pl.BlockSpec(memory_space=pl.ANY)
    scratch = [
        blocks, blocks,
        pltpu.VMEM((total, width), bf), pltpu.VMEM((total, width), bf),
        pltpu.VMEM((width, total), bf), pltpu.VMEM((width, total), bf),
        pltpu.VMEM((width, span), bf), pltpu.VMEM((width, span), bf),
        pltpu.VMEM((SLOTS, rows, total), f32), pltpu.VMEM((SLOTS, rows, total), f32),
        pltpu.VMEM((span, total), bf), pltpu.VMEM((span, total), bf),
        pltpu.VMEM((width, total), f32),
        pltpu.VMEM((rows, heads * width), bf), pltpu.VMEM((rows, heads * width), bf),
        pltpu.VMEM((SLOTS, rows, width), f32), pltpu.VMEM((SLOTS, rows, width), f32),
        blocks, blocks,
        blocks, blocks,
        pltpu.VMEM((5, rows, width), bf), pltpu.VMEM((5, rows, width), bf),
        pltpu.VMEM((rows, width), bf), pltpu.VMEM((rows, width), bf),
        pltpu.SMEM(doc_blocks.shape, jnp.int32),
        dma((3 + 2 * heads,)), dma((4,)),
        dma((11,)), dma((8,)), dma((11,)), dma((8,)),
        dma((8,)), dma((8,)), dma((5,)), dma((8,)), dma((8,)), dma((5,)),
    ]
    results = (
        jax.ShapeDtypeStruct(queries.shape, bf),
        jax.ShapeDtypeStruct(queries.shape, bf),
        jax.ShapeDtypeStruct(key_rows.shape, bf),
        jax.ShapeDtypeStruct(key_rows.shape, bf),
    )
    outputs = pl.pallas_call(
        kernel,
        out_shape=results,
        in_specs=[pl.BlockSpec(memory_space=pltpu.HBM)] * 4 + [anywhere],
        out_specs=(anywhere,) * 4,
        scratch_shapes=scratch,
        name="packed_attention",
        compiler_params=pltpu.CompilerParams(
            collective_id=0, has_side_effects=True
        ),
    )(queries, key_rows, value_rows, out_grad, doc_blocks)
    return pl.pallas_call(
        hand_on,
        out_shape=results,
        in_specs=[anywhere] * 4,
        out_specs=(anywhere,) * 4,
        scratch_shapes=[pltpu.VMEM(r.shape, r.dtype) for r in results] + [dma((2, 8))],
        name="hand_on",
    )(*outputs)


def solution(mesh):
    in_specs = (P("seq", "head"), P("seq", "head"), P("seq", "head"), P("seq", "head"), P())
    out_specs = (P("seq", "head"), P("seq", "head"), P("seq", "head"), P("seq", "head"))
    return jax.shard_map(local, mesh=mesh, in_specs=in_specs, out_specs=out_specs, check_vma=False)
```
